32 devices in a mesh: basin: 2 (over x), pair: 8 (over z, y), row: 2 (over core).
Axes of the slice: x: 2, y: 2, z: 4, core: 2. Of those that a mesh axis runs over, the one named last changes fastest.
Arguments:
- snapshots: float32 [8192, 4096], P(('basin', 'row'), 'pair'), parts along dimension 0, may hold values from -60 to 60, as said below
- plan: int32 [4, 16], replicated, may hold values from 0 to 15, as said below
Outputs:
- rotated: float32 [8192, 4096], P(('basin', 'row'), 'pair'), parts along dimension 0
The draws below stay inside these ranges and needn't reach their ends.
There are 2 independent parts, one for each index of `basin`. The reference program is written for one: setup_inputs(seed, part) draws one part's arguments, and reference() takes and returns one part's arrays. A program takes and returns all parts, laid end to end along the dimension named above; an argument that names none is the same for every part. Nothing has to cross between parts.
Inputs may be any that keep to these rules, and one draw needn't show every extreme that they name: `plan`: each row of the table is a permutation of the 16 slots. Slots 2d and 2d + 1 lie on the d-th index of pair; in every round each index sends one of its two blocks to index d + 1 and the other to index d - 1 (both modulo 8). `snapshots`: real values.
All inputs are finite; a program needn't handle non-finite values.
Results may differ from the reference program's by a relative error of at most 0.0003.
Values sent between devices are 32-bit elements; how exact they have to be, the bound alone decides.
A program may use at most 64 MiB of HBM per device.

```python
import jax
import jax.numpy as jnp
from jax import lax

B = 256
ROUNDS = 4
NS_ITERS = 6
NP = 8
M = 4096
NCOL = 4096


def draw_snapshots(key, part):
    key_rows = jax.random.fold_in(key, 11)
    key_cols = jax.random.fold_in(key, 12)
    key_vals = jax.random.fold_in(key, 13)
    col_scale = jnp.exp(jax.random.uniform(key_cols, (1, NCOL), jnp.float32, jnp.log(0.3), jnp.log(3.0)))
    row_scale = jnp.exp(jax.random.uniform(key_rows, (M, 1), jnp.float32, jnp.log(0.3), jnp.log(3.0)))
    noise = jax.random.truncated_normal(key_vals, -6.0, 6.0, (M, NCOL), jnp.float32)
    values = noise * row_scale * col_scale
    return values.astype(jnp.float32)


def draw_plan(key, part):
    key_bits = jax.random.fold_in(key, 21)
    key_order = jax.random.fold_in(key, 22)
    bits = jax.random.randint(key_bits, (ROUNDS, NP), 0, 2)
    order = jax.random.randint(key_order, (ROUNDS, NP), 0, 2)
    device = jnp.arange(NP)[None, :]
    before = jnp.roll(bits, 1, axis=1)
    after = jnp.roll(bits, -1, axis=1)
    from_below = 2 * ((device + NP - 1) % NP) + before
    from_above = 2 * ((device + 1) % NP) + 1 - after
    slot_zero = jnp.where(order == 0, from_below, from_above)
    slot_one = jnp.where(order == 0, from_above, from_below)
    return jnp.stack((slot_zero, slot_one), axis=2).reshape(ROUNDS, 2 * NP).astype(jnp.int32)


def setup_inputs(seed: int = 0, part: int = 0) -> dict:
    splits = jax.random.split(jax.random.key(seed), 3)
    own_keys = jax.random.split(jax.random.fold_in(splits[2], part), 3)
    return {
        "snapshots": draw_snapshots(jax.random.fold_in(jax.random.fold_in(splits[2], part), 71), part),
        "plan": draw_plan(jax.random.fold_in(splits[2], 71), part),
    }


epsilon = 1e-6


def reference(snapshots, plan):
    highest = lax.Precision.HIGHEST
    identity = jnp.eye(B, dtype=jnp.float32)
    field = snapshots
    for round_index in range(ROUNDS):
        blocks = field.reshape(M, NP, 2, B)
        first = blocks[:, :, 0, :]
        second = blocks[:, :, 1, :]
        cross = jnp.einsum("mpa,mpb->pab", first, second, precision=highest)
        norm_first = jnp.sum(first * first, axis=0)
        norm_second = jnp.sum(second * second, axis=0)
        coupling = cross / (norm_first[:, :, None] + norm_second[:, None, :] + epsilon)
        system = identity[None] + jnp.einsum("pab,pcb->pac", coupling, coupling, precision=highest)
        scale = 1.0 + jnp.sum(coupling * coupling, axis=(1, 2))
        inverse = identity[None] / scale[:, None, None]
        for sweep in range(NS_ITERS):
            product = jnp.einsum("pab,pbc->pac", system, inverse, precision=highest)
            inverse = jnp.einsum("pab,pbc->pac", inverse, 2.0 * identity[None] - product, precision=highest)
        lifted = first - jnp.einsum("mpb,pab->mpa", second, coupling, precision=highest)
        mixed = jnp.einsum("mpa,pac->mpc", lifted, inverse, precision=highest)
        new_first = 2.0 * mixed - first
        new_second = second + 2.0 * jnp.einsum("mpa,pab->mpb", mixed, coupling, precision=highest)
        stacked = jnp.stack((new_first, new_second), axis=2).reshape(M, 2 * NP, B)
        field = stacked[:, plan[round_index], :].reshape(M, NCOL)
    return field
```

```python
import jax
import jax.numpy as jnp
from jax import lax
from jax.experimental import pallas as pl
from jax.experimental.pallas import tpu as pltpu
from jax.sharding import PartitionSpec as P

NS_ITERS = 6
EPSILON = 1e-06
CHUNK = 128

MESH = pl.DeviceIdType.MESH
f32, bf16 = jnp.float32, jnp.bfloat16


def split(x):
    high = x.astype(bf16)
    return high, (x - high.astype(f32)).astype(bf16)


def dot(left, right, left_dim=1, right_dim=0):
    return lax.dot_general(
        left, right, (((left_dim,), (right_dim,)), ((), ())), preferred_element_type=f32
    )


def dot3(left, right, left_dim=1, right_dim=0):
    (lh, ll), (rh, rl) = left, right
    small = dot(lh, rl, left_dim, right_dim) + dot(ll, rh, left_dim, right_dim)
    return dot(lh, rh, left_dim, right_dim) + small


def inverse_of(coupling, eye):
    parts = split(coupling)
    square = dot3(parts, parts, 1, 1)
    scale = 1.0 / (1.0 + jnp.sum(coupling * coupling))
    rest = eye - (eye + square) * scale
    total = eye + rest
    power = split(rest)
    power = split(dot3(power, power))
    for step in range(NS_ITERS - 1):
        more = dot3(split(total), power)
        if step < NS_ITERS - 2:
            power = split(dot3(power, power))
        total = total + more
    return total * scale


def kernel(
    n, rounds, plan_ref, x_ref, o_ref, field, kept, recv, send, gram, other, mats,
    in_sem, out_sem, send_sem, recv_sem, gram_send, gram_recv,
):
    rows, width = kept.shape
    chunks = rows // CHUNK
    me, core = lax.axis_index("pair"), lax.axis_index("row")
    parity = lax.rem(me, 2)

    def at(c):
        return pl.ds(pl.multiple_of(c * CHUNK, CHUNK), CHUNK)

    def shift(index, k):
        return lax.rem(index + (n + k), n)

    def load(c):
        return pltpu.make_async_copy(x_ref.at[at(c)], field.at[at(c)], in_sem.at[c])

    def store(c):
        return pltpu.make_async_copy(field.at[at(c)], o_ref.at[at(c)], out_sem.at[c])

    def move(r, c):
        side = lax.rem(parity + r, 2)
        return pltpu.make_async_remote_copy(
            src_ref=send.at[r, at(c)], dst_ref=recv.at[r, at(c)],
            send_sem=send_sem.at[r, c], recv_sem=recv_sem.at[r, c],
            device_id={"pair": shift(me, 4 * side - 2)}, device_id_type=MESH,
        )

    def place(r):
        return me if r % 2 == 0 else shift(me, 1 - 2 * parity)

    def sends_second(r):
        side = lax.rem(parity + r, 2)
        here = place(r)
        goal = shift(here, 2 * side - 1)
        mine = 2 * here + 1
        return (plan_ref[r, 2 * goal] == mine) | (plan_ref[r, 2 * goal + 1] == mine)

    def first_received(r):
        side = lax.rem(parity + r, 2)
        here = place(r + 1)
        source = shift(here, 1 - 2 * side)
        got = plan_ref[r, 2 * here]
        return (got == 2 * source) | (got == 2 * source + 1)

    for c in range(chunks):
        load(c).start()

    barrier = pltpu.get_barrier_semaphore()
    for k in (2, -2):
        pl.semaphore_signal(
            barrier, inc=1, device_id={"pair": shift(me, k)}, device_id_type=MESH
        )
    pl.semaphore_signal(barrier, inc=1, device_id={"row": 1 - core}, device_id_type=MESH)

    line = lax.broadcasted_iota(jnp.int32, (width, width), 0)
    lane = lax.broadcasted_iota(jnp.int32, (width, width), 1)
    diagonal = line == lane
    eye = jnp.where(diagonal, 1.0, 0.0).astype(f32)

    for r in range(rounds):
        if r:
            flag = first_received(r - 1)

        def blocks(c, r=r):
            if r == 0:
                return field[at(c), :width], field[at(c), width:]
            old, new = kept[at(c)], recv[r - 1, at(c)]
            return jnp.where(flag, new, old), jnp.where(flag, old, new)

        gram[r] = jnp.zeros(gram.shape[1:], f32)

        def accumulate(c, _, r=r):
            if r == 0:
                load(c).wait()
            else:
                move(r - 1, c).wait_recv()
            a, b = blocks(c)
            gram[r, :width] += dot3(split(a), split(b), 0, 0)
            gram[r, width : width + 8] += jnp.sum((a * a).reshape(-1, 8, width), axis=0)
            gram[r, width + 8 :] += jnp.sum((b * b).reshape(-1, 8, width), axis=0)
            return 0

        lax.fori_loop(0, chunks, accumulate, 0)
        if r == 0:
            pl.semaphore_wait(barrier, 3)
        swap = pltpu.make_async_remote_copy(
            src_ref=gram.at[r], dst_ref=other.at[r],
            send_sem=gram_send.at[r], recv_sem=gram_recv.at[r],
            device_id={"row": 1 - core}, device_id_type=MESH,
        )
        swap.start()
        swap.wait()
        cross = gram[r, :width] + other[r, :width]
        norms = gram[r, width:] + other[r, width:]
        norm_a = jnp.sum(norms[:8], axis=0, keepdims=True)
        norm_b = jnp.sum(norms[8:], axis=0, keepdims=True)
        column = jnp.sum(jnp.where(diagonal, norm_a, 0.0), axis=1, keepdims=True)
        coupling = cross / (column + norm_b + EPSILON)
        inverse = inverse_of(coupling, eye)
        mats[0], mats[1] = split(coupling)
        mats[2], mats[3] = split(2.0 * inverse)
        choice = sends_second(r)

        def rotate(c, _, r=r):
            a, b = blocks(c)
            coupling = mats[0], mats[1]
            lifted = a - dot3(split(b), coupling, 1, 1)
            mixed = dot3(split(lifted), (mats[2], mats[3]))
            a, b = mixed - a, b + dot3(split(mixed), coupling)
            kept[at(c)] = jnp.where(choice, a, b)
            send[r, at(c)] = jnp.where(choice, b, a)
            move(r, c).start()
            return 0

        lax.fori_loop(0, chunks, rotate, 0)

    flag = first_received(rounds - 1)

    def finish(c, _):
        move(rounds - 1, c).wait_recv()
        old, new = kept[at(c)], recv[rounds - 1, at(c)]
        field[at(c), :width] = jnp.where(flag, new, old)
        field[at(c), width:] = jnp.where(flag, old, new)
        store(c).start()
        return 0

    lax.fori_loop(0, chunks, finish, 0)

    def drain(c, _):
        for r in range(rounds):
            move(r, c).wait_send()
        store(c).wait()
        return 0

    lax.fori_loop(0, chunks, drain, 0)


def solution(mesh):
    n = mesh.shape["pair"]

    def per_device(snapshots, plan):
        rounds = plan.shape[0]
        rows, width = snapshots.shape[0], snapshots.shape[1] // 2
        chunks = rows // CHUNK
        dma = pltpu.SemaphoreType.DMA

        def body(*refs):
            kernel(n, rounds, *refs)

        return pl.pallas_call(
            body,
            out_shape=jax.ShapeDtypeStruct(snapshots.shape, f32),
            in_specs=[
                pl.BlockSpec(memory_space=pltpu.SMEM),
                pl.BlockSpec(memory_space=pl.ANY),
            ],
            out_specs=pl.BlockSpec(memory_space=pl.ANY),
            scratch_shapes=[
                pltpu.VMEM((rows, 2 * width), f32),
                pltpu.VMEM((rows, width), f32),
                pltpu.VMEM((rounds, rows, width), f32),
                pltpu.VMEM((rounds, rows, width), f32),
                pltpu.VMEM((rounds, width + 16, width), f32),
                pltpu.VMEM((rounds, width + 16, width), f32),
                pltpu.VMEM((4, width, width), bf16),
                dma((chunks,)),
                dma((chunks,)),
                dma((rounds, chunks)),
                dma((rounds, chunks)),
                dma((rounds,)),
                dma((rounds,)),
            ],
            compiler_params=pltpu.CompilerParams(
                collective_id=0, has_side_effects=True, vmem_limit_bytes=48 * 2**20
            ),
            cost_estimate=pl.CostEstimate(
                flops=8 * rounds * rows * width * width,
                bytes_accessed=8 * rows * 2 * width,
                transcendentals=0,
            ),
            name="jacobi",
        )(plan, snapshots)

    in_specs = (P(("basin", "row"), "pair"), P())
    out_specs = P(("basin", "row"), "pair")
    return jax.shard_map(
        per_device, mesh=mesh, in_specs=in_specs, out_specs=out_specs, check_vma=False
    )
```

```python
import jax
import jax.numpy as jnp
from jax import lax
from jax.experimental import pallas as pl
from jax.experimental.pallas import tpu as pltpu
from jax.sharding import PartitionSpec as P

NS_ITERS = 6
EPSILON = 1e-06
CHUNK = 128
DETOURS = (4, 2), (2, 2), (2, 4)

MESH = pl.DeviceIdType.MESH
f32, bf16 = jnp.float32, jnp.bfloat16


def split(x):
    high = x.astype(bf16)
    return high, (x - high.astype(f32)).astype(bf16)


def dot(left, right, left_dim=1, right_dim=0):
    return lax.dot_general(
        left, right, (((left_dim,), (right_dim,)), ((), ())), preferred_element_type=f32
    )


def dot3(left, right, left_dim=1, right_dim=0):
    (lh, ll), (rh, rl) = left, right
    small = dot(lh, rl, left_dim, right_dim) + dot(ll, rh, left_dim, right_dim)
    return dot(lh, rh, left_dim, right_dim) + small


def inverse_of(coupling, eye):
    parts = split(coupling)
    square = dot3(parts, parts, 1, 1)
    scale = 1.0 / (1.0 + jnp.sum(coupling * coupling))
    rest = eye - (eye + square) * scale
    total = eye + rest
    power = split(rest)
    power = split(dot3(power, power))
    for step in range(NS_ITERS - 1):
        more = dot3(split(total), power)
        if step < NS_ITERS - 2:
            power = split(dot3(power, power))
        total = total + more
    return total * scale


def kernel(
    n, rounds, plan_ref, x_ref, o_ref, field, kept, recv, send, relay, gram, other, mats,
    in_sem, out_sem, send_sem, recv_sem, relay_recv, relay_send, gram_send, gram_recv,
):
    rows, width = kept.shape
    chunks = rows // CHUNK
    me, core = lax.axis_index("pair"), lax.axis_index("row")
    parity = lax.rem(me, 2)
    twin = me + 1 - 2 * parity

    def at(c):
        return pl.ds(pl.multiple_of(c * CHUNK, CHUNK), CHUNK)

    def shift(index, k):
        return lax.rem(index + (n + k), n)

    def load(c):
        return pltpu.make_async_copy(x_ref.at[at(c)], field.at[at(c)], in_sem.at[c])

    def store(c):
        return pltpu.make_async_copy(field.at[at(c)], o_ref.at[at(c)], out_sem.at[c])

    def move(r, c):
        side = lax.rem(parity + r, 2)
        return pltpu.make_async_remote_copy(
            src_ref=send.at[r, at(c)], dst_ref=recv.at[r, at(c)],
            send_sem=send_sem.at[r, c], recv_sem=recv_sem.at[r, c],
            device_id={"pair": shift(me, 4 * side - 2)}, device_id_type=MESH,
        )

    def visit(r, c):
        return pltpu.make_async_remote_copy(
            src_ref=send.at[r, at(c)], dst_ref=relay.at[r, at(c)],
            send_sem=send_sem.at[r, c], recv_sem=relay_recv.at[r, c],
            device_id={"pair": twin}, device_id_type=MESH,
        )

    def forward(r, c):
        side = lax.rem(1 - parity + r, 2)
        return pltpu.make_async_remote_copy(
            src_ref=relay.at[r, at(c)], dst_ref=recv.at[r, at(c)],
            send_sem=relay_send.at[r, c], recv_sem=recv_sem.at[r, c],
            device_id={"pair": shift(twin, 4 * side - 2)}, device_id_type=MESH,
        )

    def detour(r, side):
        even, odd = DETOURS[0 if r == 0 else 2 if r == rounds - 1 else 1]
        return chunks * (even + (odd - even) * side) // 16

    def on_turn(r, work):
        def run(turn, side):
            lax.fori_loop(0, detour(turn, 1 - side), lambda c, _: work(turn, c), 0)

        if r >= 0:
            pl.when(parity == 0)(lambda: run(r, 0))
        if r < rounds - 1:
            pl.when(parity == 1)(lambda: run(r + 1, 1))

    def pass_on(r, c):
        visit(r, c).wait_recv()
        forward(r, c).start()
        return 0

    def passed(r, c):
        forward(r, c).wait_send()
        return 0

    def place(r):
        return me if r % 2 == 0 else shift(me, 1 - 2 * parity)

    def sends_second(r):
        side = lax.rem(parity + r, 2)
        here = place(r)
        goal = shift(here, 2 * side - 1)
        mine = 2 * here + 1
        return (plan_ref[r, 2 * goal] == mine) | (plan_ref[r, 2 * goal + 1] == mine)

    def first_received(r):
        side = lax.rem(parity + r, 2)
        here = place(r + 1)
        source = shift(here, 1 - 2 * side)
        got = plan_ref[r, 2 * here]
        return (got == 2 * source) | (got == 2 * source + 1)

    for c in range(chunks):
        load(c).start()

    barrier = pltpu.get_barrier_semaphore()
    for near in (shift(me, 2), shift(me, -2), shift(twin, 2), shift(twin, -2), twin):
        pl.semaphore_signal(barrier, inc=1, device_id={"pair": near}, device_id_type=MESH)
    pl.semaphore_signal(barrier, inc=1, device_id={"row": 1 - core}, device_id_type=MESH)

    line = lax.broadcasted_iota(jnp.int32, (width, width), 0)
    lane = lax.broadcasted_iota(jnp.int32, (width, width), 1)
    diagonal = line == lane
    eye = jnp.where(diagonal, 1.0, 0.0).astype(f32)

    def in_order(r, work):
        aside = detour(r, parity)

        def both(i, _):
            work(i, 0)
            work(chunks - aside + i, 0)
            return 0

        lax.fori_loop(aside, chunks - aside, work, 0)
        lax.fori_loop(0, aside, both, 0)

    for r in range(rounds):
        if r:
            flag = first_received(r - 1)

        def blocks(c, r=r):
            if r == 0:
                return field[at(c), :width], field[at(c), width:]
            old, new = kept[at(c)], recv[r - 1, at(c)]
            return jnp.where(flag, new, old), jnp.where(flag, old, new)

        gram[r] = jnp.zeros(gram.shape[1:], f32)

        def accumulate(c, _, r=r):
            if r == 0:
                load(c).wait()
            else:
                move(r - 1, c).wait_recv()
            a, b = blocks(c)
            gram[r, :width] += dot3(split(a), split(b), 0, 0)
            gram[r, width : width + 8] += jnp.sum((a * a).reshape(-1, 8, width), axis=0)
            gram[r, width + 8 :] += jnp.sum((b * b).reshape(-1, 8, width), axis=0)
            return 0

        if r == 0:
            lax.fori_loop(0, chunks, accumulate, 0)
        else:
            in_order(r - 1, accumulate)
            on_turn(r - 1, pass_on)
        if r == 0:
            pl.semaphore_wait(barrier, 6)
        swap = pltpu.make_async_remote_copy(
            src_ref=gram.at[r], dst_ref=other.at[r],
            send_sem=gram_send.at[r], recv_sem=gram_recv.at[r],
            device_id={"row": 1 - core}, device_id_type=MESH,
        )
        swap.start()
        swap.wait()
        cross = gram[r, :width] + other[r, :width]
        norms = gram[r, width:] + other[r, width:]
        norm_a = jnp.sum(norms[:8], axis=0, keepdims=True)
        norm_b = jnp.sum(norms[8:], axis=0, keepdims=True)
        column = jnp.sum(jnp.where(diagonal, norm_a, 0.0), axis=1, keepdims=True)
        coupling = cross / (column + norm_b + EPSILON)
        inverse = inverse_of(coupling, eye)
        mats[0], mats[1] = split(coupling)
        mats[2], mats[3] = split(2.0 * inverse)
        choice = sends_second(r)

        def rotate(c, _, r=r):
            a, b = blocks(c)
            coupling = mats[0], mats[1]
            lifted = a - dot3(split(b), coupling, 1, 1)
            mixed = dot3(split(lifted), (mats[2], mats[3]))
            a, b = mixed - a, b + dot3(split(mixed), coupling)
            kept[at(c)] = jnp.where(choice, a, b)
            send[r, at(c)] = jnp.where(choice, b, a)
            return 0

        def direct(c, _, r=r):
            rotate(c, 0)
            move(r, c).start()
            return 0

        def aside(c, _, r=r):
            rotate(c, 0)
            visit(r, c).start()
            return 0

        count = detour(r, parity)
        done = 0
        if r == 0:
            @pl.when(parity == 1)
            def _(count=count):
                direct(count, 0)

            done = parity
            on_turn(-1, pass_on)
        on_turn(r - 1, passed)

        def both(i, _):
            direct(count + done + i, 0)
            aside(i, 0)
            return 0

        lax.fori_loop(0, count, both, 0)
        lax.fori_loop(2 * count + done, chunks, direct, 0)

    flag = first_received(rounds - 1)

    def finish(c, _):
        move(rounds - 1, c).wait_recv()
        old, new = kept[at(c)], recv[rounds - 1, at(c)]
        field[at(c), :width] = jnp.where(flag, new, old)
        field[at(c), width:] = jnp.where(flag, old, new)
        store(c).start()
        return 0

    in_order(rounds - 1, finish)
    on_turn(rounds - 1, pass_on)
    on_turn(rounds - 1, passed)

    def drain(c, _):
        for r in range(rounds):
            move(r, c).wait_send()
        store(c).wait()
        return 0

    lax.fori_loop(0, chunks, drain, 0)


def solution(mesh):
    n = mesh.shape["pair"]

    def per_device(snapshots, plan):
        rounds = plan.shape[0]
        rows, width = snapshots.shape[0], snapshots.shape[1] // 2
        chunks = rows // CHUNK
        detour = chunks * max(map(max, DETOURS)) // 16
        dma = pltpu.SemaphoreType.DMA

        def body(*refs):
            kernel(n, rounds, *refs)

        return pl.pallas_call(
            body,
            out_shape=jax.ShapeDtypeStruct(snapshots.shape, f32),
            in_specs=[
                pl.BlockSpec(memory_space=pltpu.SMEM),
                pl.BlockSpec(memory_space=pl.ANY),
            ],
            out_specs=pl.BlockSpec(memory_space=pl.ANY),
            scratch_shapes=[
                pltpu.VMEM((rows, 2 * width), f32),
                pltpu.VMEM((rows, width), f32),
                pltpu.VMEM((rounds, rows, width), f32),
                pltpu.VMEM((rounds, rows, width), f32),
                pltpu.VMEM((rounds, detour * CHUNK, width), f32),
                pltpu.VMEM((rounds, width + 16, width), f32),
                pltpu.VMEM((rounds, width + 16, width), f32),
                pltpu.VMEM((4, width, width), bf16),
                dma((chunks,)),
                dma((chunks,)),
                dma((rounds, chunks)),
                dma((rounds, chunks)),
                dma((rounds, detour)),
                dma((rounds, detour)),
                dma((rounds,)),
                dma((rounds,)),
            ],
            compiler_params=pltpu.CompilerParams(
                collective_id=0, has_side_effects=True, vmem_limit_bytes=48 * 2**20
            ),
            cost_estimate=pl.CostEstimate(
                flops=8 * rounds * rows * width * width,
                bytes_accessed=8 * rows * 2 * width,
                transcendentals=0,
            ),
            name="jacobi",
        )(plan, snapshots)

    in_specs = (P(("basin", "row"), "pair"), P())
    out_specs = P(("basin", "row"), "pair")
    return jax.shard_map(
        per_device, mesh=mesh, in_specs=in_specs, out_specs=out_specs, check_vma=False
    )
```

```python
import jax
import jax.numpy as jnp
from jax import lax
from jax.experimental import pallas as pl
from jax.experimental.pallas import tpu as pltpu
from jax.sharding import PartitionSpec as P

NS_ITERS = 6
EPSILON = 1e-06
CHUNK = 128
GROUP = 4
DETOURS = (5, 3), (3, 3), (3, 5)

MESH = pl.DeviceIdType.MESH
f32, bf16 = jnp.float32, jnp.bfloat16


def split(x):
    high = x.astype(bf16)
    return high, (x - high.astype(f32)).astype(bf16)


def dot(left, right, left_dim=1, right_dim=0):
    return lax.dot_general(
        left, right, (((left_dim,), (right_dim,)), ((), ())), preferred_element_type=f32
    )


def dot3(left, right, left_dim=1, right_dim=0):
    (lh, ll), (rh, rl) = left, right
    small = dot(lh, rl, left_dim, right_dim) + dot(ll, rh, left_dim, right_dim)
    return dot(lh, rh, left_dim, right_dim) + small


def stack_left(x):
    high, low = split(x)
    return jnp.concatenate([high, high, low], axis=1)


def stack_right(x):
    high, low = split(x)
    return jnp.concatenate([high, low, high], axis=0)


def gram_of(a, b):
    ah, al = split(a)
    return dot(jnp.concatenate([ah, ah, al], axis=0), stack_right(b), 0, 0)


def inverse_of(coupling, eye):
    parts = split(coupling)
    square = dot3(parts, parts, 1, 1)
    scale = 1.0 / (1.0 + jnp.sum(coupling * coupling))
    rest = eye - (eye + square) * scale
    total = eye + rest
    power = split(rest)
    power = split(dot3(power, power))
    for step in range(NS_ITERS - 1):
        more = dot3(split(total), power)
        if step < NS_ITERS - 2:
            power = split(dot3(power, power))
        total = total + more
    return total * scale


def kernel(
    n, rounds, plan_hbm, x_ref, o_ref, plan_ref, field, kept, recv, send, relay, gram, other, mats,
    plan_sem, in_sem, out_sem, send_sem, recv_sem, relay_recv, relay_send, gram_send, gram_recv,
):
    rows, width = kept.shape
    chunks = rows // CHUNK
    me, core = lax.axis_index("pair"), lax.axis_index("row")
    parity = lax.rem(me, 2)
    twin = me + 1 - 2 * parity

    def at(c):
        return pl.ds(pl.multiple_of(c * CHUNK, CHUNK), CHUNK)

    def shift(index, k):
        return lax.rem(index + (n + k), n)

    def load(c):
        return pltpu.make_async_copy(x_ref.at[at(c)], field.at[at(c)], in_sem.at[c])

    def store(c):
        return pltpu.make_async_copy(field.at[at(c)], o_ref.at[at(c)], out_sem.at[c])

    def move(r, c):
        return pltpu.make_async_remote_copy(
            src_ref=send.at[r, at(c)], dst_ref=recv.at[r, at(c)],
            send_sem=send_sem.at[r, c], recv_sem=recv_sem.at[r, c],
            device_id={"pair": shift(me, r % 2 * 4 - 2)}, device_id_type=MESH,
        )

    def visit(r, c):
        return pltpu.make_async_remote_copy(
            src_ref=send.at[r, at(c)], dst_ref=relay.at[r, at(c)],
            send_sem=send_sem.at[r, c], recv_sem=relay_recv.at[r, c],
            device_id={"pair": twin}, device_id_type=MESH,
        )

    def forward(r, c):
        return pltpu.make_async_remote_copy(
            src_ref=relay.at[r, at(c)], dst_ref=recv.at[r, at(c)],
            send_sem=relay_send.at[r, c], recv_sem=recv_sem.at[r, c],
            device_id={"pair": shift(twin, r % 2 * 4 - 2)}, device_id_type=MESH,
        )

    def detour(r, side):
        even, odd = DETOURS[0 if r == 0 else 2 if r == rounds - 1 else 1]
        return chunks * (even + (odd - even) * side) // 16

    def on_turn(r, work):
        def run(turn, side):
            lax.fori_loop(0, detour(turn, 1 - side), lambda c, _: work(turn, c), 0)

        if r >= 0:
            pl.when(parity == 0)(lambda: run(r, 0))
        if r < rounds - 1:
            pl.when(parity == 1)(lambda: run(r + 1, 1))

    def pass_on(r, c):
        visit(r, c).wait_recv()
        forward(r, c).start()
        return 0

    def passed(r, c):
        forward(r, c).wait_send()
        return 0

    def place(r):
        return me if r % 2 == 0 else shift(me, 1)

    def sends_second(r):
        side = r % 2
        here = place(r)
        goal = shift(here, 2 * side - 1)
        mine = 2 * here + 1
        return (plan_ref[r, 2 * goal] == mine) | (plan_ref[r, 2 * goal + 1] == mine)

    def first_received(r):
        side = r % 2
        here = place(r + 1)
        source = shift(here, 1 - 2 * side)
        got = plan_ref[r, 2 * here]
        return (got == 2 * source) | (got == 2 * source + 1)

    for c in range(chunks):
        load(c).start()
    layout = pltpu.make_async_copy(plan_hbm, plan_ref, plan_sem)
    layout.start()

    barrier = pltpu.get_barrier_semaphore()
    for near in (shift(me, 2), shift(me, -2), shift(twin, 2), shift(twin, -2), twin):
        pl.semaphore_signal(barrier, inc=1, device_id={"pair": near}, device_id_type=MESH)
    pl.semaphore_signal(barrier, inc=1, device_id={"row": 1 - core}, device_id_type=MESH)

    line = lax.broadcasted_iota(jnp.int32, (width, width), 0)
    lane = lax.broadcasted_iota(jnp.int32, (width, width), 1)
    diagonal = line == lane
    eye = jnp.where(diagonal, 1.0, 0.0).astype(f32)

    def in_order(r, work):
        aside = detour(r, parity)

        def both(i, _):
            work(i, 0)
            work(chunks - aside + i, 0)
            return 0

        lax.fori_loop(aside, chunks - aside, work, 0)
        lax.fori_loop(0, aside, both, 0)

    for r in range(rounds):
        if r:
            flag = first_received(r - 1)

        def blocks(c, r=r):
            if r == 0:
                return field[at(c), :width], field[at(c), width:]
            old, new = kept[at(c)], recv[r - 1, at(c)]
            return jnp.where(flag, new, old), jnp.where(flag, old, new)

        gram[r] = jnp.zeros(gram.shape[1:], f32)

        def accumulate(a, b, r=r):
            gram[r, :width] += gram_of(a, b)
            gram[r, width : width + 8] += jnp.sum((a * a).reshape(-1, 8, width), axis=0)
            gram[r, width + 8 :] += jnp.sum((b * b).reshape(-1, 8, width), axis=0)

        def arrived(c, _, r=r):
            move(r - 1, c).wait_recv()
            accumulate(*blocks(c))
            return 0

        def loaded(g, _):
            for k in range(GROUP):
                load(g * GROUP + k).wait()
            part = pl.ds(pl.multiple_of(g * GROUP * CHUNK, CHUNK), GROUP * CHUNK)
            accumulate(field[part, :width], field[part, width:])
            return 0

        if r == 0:
            lax.fori_loop(0, chunks // GROUP, loaded, 0)
        else:
            in_order(r - 1, arrived)
            on_turn(r - 1, pass_on)
        if r == 0:
            pl.semaphore_wait(barrier, 6)
            layout.wait()
        swap = pltpu.make_async_remote_copy(
            src_ref=gram.at[r], dst_ref=other.at[r],
            send_sem=gram_send.at[r], recv_sem=gram_recv.at[r],
            device_id={"row": 1 - core}, device_id_type=MESH,
        )
        swap.start()
        swap.wait()
        cross = gram[r, :width] + other[r, :width]
        norms = gram[r, width:] + other[r, width:]
        norm_a = jnp.sum(norms[:8], axis=0, keepdims=True)
        norm_b = jnp.sum(norms[8:], axis=0, keepdims=True)
        column = jnp.sum(jnp.where(diagonal, norm_a, 0.0), axis=1, keepdims=True)
        coupling = cross / (column + norm_b + EPSILON)
        inverse = inverse_of(coupling, eye)
        mats[0] = stack_right(coupling.T)
        mats[1] = stack_right(2.0 * inverse)
        mats[2] = stack_right(coupling)
        choice = sends_second(r)

        def rotate(c, _, r=r):
            a, b = blocks(c)
            lifted = a - dot(stack_left(b), mats[0])
            mixed = dot(stack_left(lifted), mats[1])
            a, b = mixed - a, b + dot(stack_left(mixed), mats[2])
            kept[at(c)] = jnp.where(choice, a, b)
            send[r, at(c)] = jnp.where(choice, b, a)
            return 0

        def direct(c, _, r=r):
            rotate(c, 0)
            move(r, c).start()
            return 0

        def aside(c, _, r=r):
            rotate(c, 0)
            visit(r, c).start()
            return 0

        count = detour(r, parity)
        if r == 0:
            direct(count, 0)
        lax.fori_loop(0, count, aside, 0)
        if r == 0:
            on_turn(-1, pass_on)
        on_turn(r - 1, passed)
        lax.fori_loop(count + (r == 0), chunks, direct, 0)

    flag = first_received(rounds - 1)

    def finish(c, _):
        move(rounds - 1, c).wait_recv()
        old, new = kept[at(c)], recv[rounds - 1, at(c)]
        field[at(c), :width] = jnp.where(flag, new, old)
        field[at(c), width:] = jnp.where(flag, old, new)
        store(c).start()
        return 0

    in_order(rounds - 1, finish)
    on_turn(rounds - 1, pass_on)
    on_turn(rounds - 1, passed)

    def drain(c, _):
        for r in range(rounds):
            move(r, c).wait_send()
        store(c).wait()
        return 0

    lax.fori_loop(0, chunks, drain, 0)


def solution(mesh):
    n = mesh.shape["pair"]

    def per_device(snapshots, plan):
        rounds = plan.shape[0]
        rows, width = snapshots.shape[0], snapshots.shape[1] // 2
        chunks = rows // CHUNK
        detour = chunks * max(map(max, DETOURS)) // 16
        dma = pltpu.SemaphoreType.DMA

        def body(*refs):
            kernel(n, rounds, *refs)

        return pl.pallas_call(
            body,
            out_shape=jax.ShapeDtypeStruct(snapshots.shape, f32),
            in_specs=[
                pl.BlockSpec(memory_space=pl.ANY),
                pl.BlockSpec(memory_space=pl.ANY),
            ],
            out_specs=pl.BlockSpec(memory_space=pl.ANY),
            scratch_shapes=[
                pltpu.SMEM(plan.shape, jnp.int32),
                pltpu.VMEM((rows, 2 * width), f32),
                pltpu.VMEM((rows, width), f32),
                pltpu.VMEM((rounds, rows, width), f32),
                pltpu.VMEM((rounds, rows, width), f32),
                pltpu.VMEM((rounds, detour * CHUNK, width), f32),
                pltpu.VMEM((rounds, width + 16, width), f32),
                pltpu.VMEM((rounds, width + 16, width), f32),
                pltpu.VMEM((3, 3 * width, width), bf16),
                dma,
                dma((chunks,)),
                dma((chunks,)),
                dma((rounds, chunks)),
                dma((rounds, chunks)),
                dma((rounds, detour)),
                dma((rounds, detour)),
                dma((rounds,)),
                dma((rounds,)),
            ],
            compiler_params=pltpu.CompilerParams(
                collective_id=0, has_side_effects=True, vmem_limit_bytes=48 * 2**20
            ),
            cost_estimate=pl.CostEstimate(
                flops=8 * rounds * rows * width * width,
                bytes_accessed=8 * rows * 2 * width,
                transcendentals=0,
            ),
            name="jacobi",
        )(plan, snapshots)

    in_specs = (P(("basin", "row"), "pair"), P())
    out_specs = P(("basin", "row"), "pair")
    return jax.shard_map(
        per_device, mesh=mesh, in_specs=in_specs, out_specs=out_specs, check_vma=False
    )
```

```python
import jax
import jax.numpy as jnp
from jax import lax
from jax.experimental import pallas as pl
from jax.experimental.pallas import tpu as pltpu
from jax.sharding import PartitionSpec as P

NS_ITERS = 6
EPSILON = 1e-06
CHUNK = 128
GROUP = 4
DETOURS = (5, 3), (3, 3), (3, 5)

MESH = pl.DeviceIdType.MESH
f32, bf16 = jnp.float32, jnp.bfloat16


def split(x):
    high = x.astype(bf16)
    return high, (x - high.astype(f32)).astype(bf16)


def dot(left, right, left_dim=1, right_dim=0):
    return lax.dot_general(
        left, right, (((left_dim,), (right_dim,)), ((), ())), preferred_element_type=f32
    )


def dot3(left, right, left_dim=1, right_dim=0):
    (lh, ll), (rh, rl) = left, right
    small = dot(lh, rl, left_dim, right_dim) + dot(ll, rh, left_dim, right_dim)
    return dot(lh, rh, left_dim, right_dim) + small


def stack_left(x):
    high, low = split(x)
    return jnp.concatenate([high, high, low], axis=1)


def stack_right(x):
    high, low = split(x)
    return jnp.concatenate([high, low, high], axis=0)


def gram_of(a, b):
    ah, al = split(a)
    return dot(jnp.concatenate([ah, ah, al], axis=0), stack_right(b), 0, 0)


def inverse_of(coupling, eye):
    parts = split(coupling)
    square = dot3(parts, parts, 1, 1)
    scale = 1.0 / (1.0 + jnp.sum(coupling * coupling))
    rest = eye - (eye + square) * scale
    total = eye + rest
    power = split(rest)
    power = split(dot3(power, power))
    for step in range(NS_ITERS - 1):
        more = dot3(split(total), power)
        if step < NS_ITERS - 2:
            power = split(dot3(power, power))
        total = total + more
    return total * scale


def kernel(
    n, rounds, plan_hbm, x_ref, o_ref, plan_ref, field, kept, recv, send, relay, gram, other, mats,
    plan_sem, in_sem, out_sem, send_sem, recv_sem, relay_recv, relay_send, gram_send, gram_recv,
):
    rows, width = kept.shape
    chunks = rows // CHUNK
    me, core = lax.axis_index("pair"), lax.axis_index("row")
    parity = lax.rem(me, 2)
    twin = me + 1 - 2 * parity

    def at(c):
        return pl.ds(pl.multiple_of(c * CHUNK, CHUNK), CHUNK)

    def shift(index, k):
        return lax.rem(index + (n + k), n)

    def load(c):
        return pltpu.make_async_copy(x_ref.at[at(c)], field.at[at(c)], in_sem.at[c])

    def store(c):
        return pltpu.make_async_copy(field.at[at(c)], o_ref.at[at(c)], out_sem.at[c])

    def move(r, c):
        return pltpu.make_async_remote_copy(
            src_ref=send.at[r, at(c)], dst_ref=recv.at[r, at(c)],
            send_sem=send_sem.at[r, c], recv_sem=recv_sem.at[r, c],
            device_id={"pair": shift(me, r % 2 * 4 - 2)}, device_id_type=MESH,
        )

    def visit(r, c):
        return pltpu.make_async_remote_copy(
            src_ref=send.at[r, at(c)], dst_ref=relay.at[r, at(c)],
            send_sem=send_sem.at[r, c], recv_sem=relay_recv.at[r, c],
            device_id={"pair": twin}, device_id_type=MESH,
        )

    def forward(r, c):
        return pltpu.make_async_remote_copy(
            src_ref=relay.at[r, at(c)], dst_ref=recv.at[r, at(c)],
            send_sem=relay_send.at[r, c], recv_sem=recv_sem.at[r, c],
            device_id={"pair": shift(twin, r % 2 * 4 - 2)}, device_id_type=MESH,
        )

    def detour(r, side):
        even, odd = DETOURS[0 if r == 0 else 2 if r == rounds - 1 else 1]
        return chunks * (even + (odd - even) * side) // 16

    def on_turn(r, work):
        def run(turn, side):
            lax.fori_loop(0, detour(turn, 1 - side), lambda c, _: work(turn, c), 0)

        if r >= 0:
            pl.when(parity == 0)(lambda: run(r, 0))
        if r < rounds - 1:
            pl.when(parity == 1)(lambda: run(r + 1, 1))

    def pass_on(r, c):
        visit(r, c).wait_recv()
        forward(r, c).start()
        return 0

    def passed(r, c):
        forward(r, c).wait_send()
        return 0

    def place(r):
        return me if r % 2 == 0 else shift(me, 1)

    def sends_second(r):
        side = r % 2
        here = place(r)
        goal = shift(here, 2 * side - 1)
        mine = 2 * here + 1
        return (plan_ref[r, 2 * goal] == mine) | (plan_ref[r, 2 * goal + 1] == mine)

    def first_received(r):
        side = r % 2
        here = place(r + 1)
        source = shift(here, 1 - 2 * side)
        got = plan_ref[r, 2 * here]
        return (got == 2 * source) | (got == 2 * source + 1)

    for c in range(chunks):
        load(c).start()
    layout = pltpu.make_async_copy(plan_hbm, plan_ref, plan_sem)
    layout.start()

    barrier = pltpu.get_barrier_semaphore()
    for near in (shift(me, 2), shift(me, -2), shift(twin, 2), shift(twin, -2), twin):
        pl.semaphore_signal(barrier, inc=1, device_id={"pair": near}, device_id_type=MESH)
    pl.semaphore_signal(barrier, inc=1, device_id={"row": 1 - core}, device_id_type=MESH)

    line = lax.broadcasted_iota(jnp.int32, (width, width), 0)
    lane = lax.broadcasted_iota(jnp.int32, (width, width), 1)
    diagonal = line == lane
    eye = jnp.where(diagonal, 1.0, 0.0).astype(f32)

    def in_order(r, work):
        aside = detour(r, parity)

        def both(i, _):
            work(i, 0)
            work(chunks - aside + i, 0)
            return 0

        lax.fori_loop(aside, chunks - aside, work, 0)
        lax.fori_loop(0, aside, both, 0)

    for r in range(rounds):
        if r:
            flag = first_received(r - 1)

        def blocks(c, r=r):
            if r == 0:
                return field[at(c), :width], field[at(c), width:]
            old, new = kept[at(c)], recv[r - 1, at(c)]
            return jnp.where(flag, new, old), jnp.where(flag, old, new)

        gram[r] = jnp.zeros(gram.shape[1:], f32)

        def accumulate(a, b, r=r):
            gram[r, :width] += gram_of(a, b)
            gram[r, width : width + 8] += jnp.sum((a * a).reshape(-1, 8, width), axis=0)
            gram[r, width + 8 :] += jnp.sum((b * b).reshape(-1, 8, width), axis=0)

        def arrived(c, _, r=r):
            move(r - 1, c).wait_recv()
            accumulate(*blocks(c))
            return 0

        def loaded(g, _):
            for k in range(GROUP):
                load(g * GROUP + k).wait()
            part = pl.ds(pl.multiple_of(g * GROUP * CHUNK, CHUNK), GROUP * CHUNK)
            accumulate(field[part, :width], field[part, width:])
            return 0

        if r == 0:
            lax.fori_loop(0, chunks // GROUP, loaded, 0)
        else:
            in_order(r - 1, arrived)
            on_turn(r - 1, pass_on)
        if r == 0:
            pl.semaphore_wait(barrier, 6)
            layout.wait()
        swap = pltpu.make_async_remote_copy(
            src_ref=gram.at[r], dst_ref=other.at[r],
            send_sem=gram_send.at[r], recv_sem=gram_recv.at[r],
            device_id={"row": 1 - core}, device_id_type=MESH,
        )
        swap.start()
        swap.wait()
        cross = gram[r, :width] + other[r, :width]
        norms = gram[r, width:] + other[r, width:]
        norm_a = jnp.sum(norms[:8], axis=0, keepdims=True)
        norm_b = jnp.sum(norms[8:], axis=0, keepdims=True)
        column = jnp.sum(jnp.where(diagonal, norm_a, 0.0), axis=1, keepdims=True)
        coupling = cross / (column + norm_b + EPSILON)
        inverse = inverse_of(coupling, eye)
        mats[0] = stack_right(coupling.T)
        mats[1] = stack_right(2.0 * inverse)
        mats[2] = stack_right(coupling)
        choice = sends_second(r)

        def rotate(c, _, r=r):
            a, b = blocks(c)
            lifted = a - dot(stack_left(b), mats[0])
            mixed = dot(stack_left(lifted), mats[1])
            a, b = mixed - a, b + dot(stack_left(mixed), mats[2])
            kept[at(c)] = jnp.where(choice, a, b)
            send[r, at(c)] = jnp.where(choice, b, a)
            return 0

        def direct(c, _, r=r):
            rotate(c, 0)
            move(r, c).start()
            return 0

        def aside(c, _, r=r):
            rotate(c, 0)
            visit(r, c).start()
            return 0

        count = detour(r, parity)
        if r == 0:
            direct(count, 0)
        lax.fori_loop(0, count, aside, 0)
        if r == 0:
            on_turn(-1, pass_on)
        on_turn(r - 1, passed)
        lax.fori_loop(count + (r == 0), chunks, direct, 0)

    flag = first_received(rounds - 1)

    def finish(c, _):
        move(rounds - 1, c).wait_recv()
        old, new = kept[at(c)], recv[rounds - 1, at(c)]
        field[at(c), :width] = jnp.where(flag, new, old)
        field[at(c), width:] = jnp.where(flag, old, new)
        store(c).start()
        return 0

    in_order(rounds - 1, finish)
    on_turn(rounds - 1, pass_on)
    on_turn(rounds - 1, passed)

    def drain(c, _):
        for r in range(rounds):
            move(r, c).wait_send()
        store(c).wait()
        return 0

    lax.fori_loop(0, chunks, drain, 0)


def solution(mesh):
    n = mesh.shape["pair"]

    def per_device(snapshots, plan):
        rounds = plan.shape[0]
        rows, width = snapshots.shape[0], snapshots.shape[1] // 2
        chunks = rows // CHUNK
        detour = chunks * max(map(max, DETOURS)) // 16
        dma = pltpu.SemaphoreType.DMA

        def body(*refs):
            kernel(n, rounds, *refs)

        return pl.pallas_call(
            body,
            out_shape=jax.ShapeDtypeStruct(snapshots.shape, f32),
            in_specs=[
                pl.BlockSpec(memory_space=pl.ANY),
                pl.BlockSpec(memory_space=pl.ANY),
            ],
            out_specs=pl.BlockSpec(memory_space=pl.ANY),
            scratch_shapes=[
                pltpu.SMEM(plan.shape, jnp.int32),
                pltpu.VMEM((rows, 2 * width), f32),
                pltpu.VMEM((rows, width), f32),
                pltpu.VMEM((rounds, rows, width), f32),
                pltpu.VMEM((rounds, rows, width), f32),
                pltpu.VMEM((rounds, detour * CHUNK, width), f32),
                pltpu.VMEM((rounds, width + 16, width), f32),
                pltpu.VMEM((rounds, width + 16, width), f32),
                pltpu.VMEM((3, 3 * width, width), bf16),
                dma,
                dma((chunks,)),
                dma((chunks,)),
                dma((rounds, chunks)),
                dma((rounds, chunks)),
                dma((rounds, detour)),
                dma((rounds, detour)),
                dma((rounds,)),
                dma((rounds,)),
            ],
            compiler_params=pltpu.CompilerParams(
                collective_id=0, has_side_effects=True, vmem_limit_bytes=48 * 2**20
            ),
            cost_estimate=pl.CostEstimate(
                flops=8 * rounds * rows * width * width,
                bytes_accessed=8 * rows * 2 * width,
                transcendentals=0,
            ),
            name="jacobi",
        )(
            pltpu.with_memory_space_constraint(plan, pltpu.HBM),
            pltpu.with_memory_space_constraint(snapshots, pltpu.HBM),
        )

    in_specs = (P(("basin", "row"), "pair"), P())
    out_specs = P(("basin", "row"), "pair")
    return jax.shard_map(
        per_device, mesh=mesh, in_specs=in_specs, out_specs=out_specs, check_vma=False
    )
```
